32 devices in a mesh: wide: 8 (over y, x, core), narrow: 4 (over z).
Axes of the slice: x: 2, y: 2, z: 4, core: 2. Of those that a mesh axis runs over, the one named last changes fastest.
Arguments:
- positions: float32 [3, 4096], P(None, ('wide', 'narrow')), may hold values from 0 to 8, as said below
- features: float32 [4096, 256], P(('wide', 'narrow')), may hold values from -6 to 6
- block_counts: int32 [8], P('wide'), may hold values from 2 to 4, as said below
- pair_list: int32 [8, 4, 3, 4], P('wide', 'narrow'), may hold values from 0 to 3, as said below
- pair_count: int32 [8, 4], P('wide', 'narrow'), may hold values from 0 to 4, as said below
- pair_mask: int32 [8, 4, 4, 128, 128], P('wide', 'narrow'), may hold values 0 or 1
- w_rbf: float32 [16, 256], replicated, may hold values from -0.125 to 0.125
- wavevectors: float32 [3, 2048], P(None, 'narrow'), may hold values from -3 to 3
- kfilter: float32 [2048, 256], P('narrow'), may hold values from 1 to 30
- w_in: bfloat16 [256, 512], replicated, may hold values from -0.375 to 0.375
- w_out: bfloat16 [512, 256], replicated, may hold values from -0.25 to 0.25
Outputs:
- updated: float32 [4096, 256], P(('wide', 'narrow'))
The draws below stay inside these ranges and needn't reach their ends.
Inputs may be any that keep to these rules, and one draw needn't show every extreme that they name: `positions`: atoms of slab s have their first coordinate in [s, s + 1), the other two in [0, 1). The live blocks of a slab are its first block_counts ones; some slab and the next one both hold 4 live blocks. `pair_list`: slots below pair_count of a device are valid, the rest hold zeros. Row 0 is a local block of the device (below 1), row 1 the slab offset (0: own slab, 1: next slab), row 2 a block of that slab (below 4); both blocks are live; with offset 0 the peer block's index in the slab is greater than the own block's; each unordered block pair appears in at most one valid slot of all devices. `pair_count`: some device lists 4 pairs.
All inputs are finite; a program needn't handle non-finite values. No bound on the sum of `pair_mask` on one device may be relied on, other than what follows from the above.
Results may differ from the reference program's by a relative error of at most 0.005.
Values sent between devices are 32-bit elements; how exact they have to be, the bound alone decides.
A program may use at most 64 MiB of HBM per device.

```python
import math
import jax
import jax.numpy as jnp
from jax import lax

C = 256
HID = 512
RBF = 16
K = 2048
BLOCK = 128
BLK_DEV = 1
SLAB_BLOCKS = 4
SLAB = 512
ATOMS = 4096
MAXP = 4
N_WIDE = 8
N_NARROW = 4


def live_counts(key):
    drawn = jax.random.randint(jax.random.fold_in(key, 11), (N_WIDE,), SLAB_BLOCKS // 2, SLAB_BLOCKS + 1)
    first_full = jax.random.randint(jax.random.fold_in(key, 12), (), 0, N_WIDE - 1)
    slab_index = jnp.arange(N_WIDE)
    is_full = (slab_index == first_full) | (slab_index == first_full + 1)
    return jnp.where(is_full, SLAB_BLOCKS, drawn).astype(jnp.int32)


def pair_table(key):
    counts = live_counts(key)
    next_counts = jnp.concatenate([counts[1:], jnp.zeros((1,), jnp.int32)])
    slab_index = jnp.arange(N_WIDE)[:, None, None, None]
    narrow_index = jnp.arange(N_NARROW)[None, :, None, None]
    local_block = jnp.arange(BLK_DEV)[None, None, :, None]
    candidate = jnp.arange(4)[None, None, None, :]
    own_block = narrow_index * BLK_DEV + local_block
    offsets = jnp.where(candidate == 0, 0, 1)
    peer_block = jnp.where(candidate == 0, own_block + 1, own_block + candidate - 2)
    own_count = counts[slab_index]
    limit_count = jnp.where(offsets == 0, own_count, next_counts[slab_index])
    usable = (own_block < own_count) & (peer_block >= 0) & (peer_block < limit_count)
    full_shape = (N_WIDE, N_NARROW, BLK_DEV, 4)
    flat_shape = (N_WIDE, N_NARROW, MAXP)
    usable = jnp.broadcast_to(usable, full_shape).reshape(flat_shape)
    columns = [jnp.broadcast_to(member, full_shape).reshape(flat_shape) for member in (local_block, offsets, peer_block)]
    ranking = jnp.argsort(jnp.where(usable, 0, 1).astype(jnp.int32), axis=-1, stable=True)
    kept = jnp.take_along_axis(usable, ranking, axis=-1).astype(jnp.int32)
    sorted_cols = [jnp.take_along_axis(column, ranking, axis=-1) * kept for column in columns]
    table = jnp.stack(sorted_cols, axis=2).astype(jnp.int32)
    return (table, jnp.sum(usable.astype(jnp.int32), axis=-1).astype(jnp.int32))


def draw_block_counts(key, part):
    return live_counts(key)


def draw_pair_list(key, part):
    return pair_table(key)[0]


def draw_pair_count(key, part):
    return pair_table(key)[1]


def draw_positions(key, part):
    slab_of = (jnp.arange(ATOMS) // SLAB).astype(jnp.float32)
    fraction = jax.random.uniform(jax.random.fold_in(key, 21), (3, ATOMS), jnp.float32)
    across_slabs = slab_of + fraction[0]
    return jnp.concatenate([across_slabs[None, :], fraction[1:]], axis=0).astype(jnp.float32)


def place_ends(array, key, low, high):
    longest = array.shape.index(max(array.shape))
    spots = []
    for shift in (0, 1):
        where = [jax.random.randint(jax.random.fold_in(key, axis), (), 0, length) for axis, length in enumerate(array.shape)]
        where[longest] = (where[longest] + shift) % array.shape[longest]
        spots.append(tuple(where))
    return array.at[spots[0]].set(low).at[spots[1]].set(high)


def block_scale(key, dims, split, low, largest):
    def one(position, shards_of):
        steps = jax.random.uniform(jax.random.fold_in(jax.random.fold_in(key, 6), position), (shards_of,), jnp.float32, low / len(split), largest / len(split))
        return jnp.repeat(jnp.exp(steps), dims[position] // shards_of).reshape((-1,) + (1,) * (len(dims) - position - 1))

    gain = one(*split[0])
    for cut in split[1:]:
        gain = gain * one(*cut)
    return gain


def centred(rng, shape, deviation, bound, shards=(), kind=jnp.bfloat16):
    entries = deviation * jax.random.normal(rng, shape, jnp.float32)
    if shards:
        entries = entries * block_scale(rng, shape, shards, -0.22, 0.18)
    return jnp.clip(entries, -bound, bound).astype(kind)


def setup_inputs(seed: int = 0) -> dict:
    keys = jax.random.split(jax.random.key(seed), 12)
    positions = draw_positions(jax.random.fold_in(keys[11], 71), 0)
    features = centred(keys[1], (ATOMS, C), 1.0, 6.0, ((0, 32),), jnp.float32)
    block_counts = draw_block_counts(jax.random.fold_in(keys[11], 71), 0)
    pair_list = draw_pair_list(jax.random.fold_in(keys[11], 71), 0)
    pair_count = draw_pair_count(jax.random.fold_in(keys[11], 71), 0)
    pair_mask = place_ends((jax.random.randint(keys[5], (N_WIDE, N_NARROW, MAXP, BLOCK, BLOCK), 0, 3) < 1).astype(jnp.int32), jax.random.fold_in(keys[5], 1), 0, 1)
    w_rbf = centred(keys[6], (RBF, C), (RBF * BLOCK) ** -0.5, 0.125, (), jnp.float32)
    wavevectors = jnp.clip(jax.random.uniform(keys[7], (3, K), jnp.float32, -3.0, 3.0) * block_scale(keys[7], (3, K), ((1, 4),), -0.4, 0.0), -3.0, 3.0)
    kfilter = jnp.clip(jnp.exp(math.log(30.0) - 3.4011974 * jax.random.uniform(keys[8], (K, C), jnp.float32) ** block_scale(keys[8], (K, C), ((0, 4),), -0.2, 0.2)), 1.0, 30.0)
    w_in = centred(keys[9], (C, HID), C ** -0.5, 0.375)
    w_out = centred(keys[10], (HID, C), HID ** -0.5, 0.25)
    return {"positions": positions, "features": features, "block_counts": block_counts, "pair_list": pair_list, "pair_count": pair_count, "pair_mask": pair_mask, "w_rbf": w_rbf, "wavevectors": wavevectors, "kfilter": kfilter, "w_in": w_in, "w_out": w_out}


cutoff = 2.0
sigma_width = 0.25

def radial_filters(own_pos, peer_pos, mask_values):
    delta_x = own_pos[0][:, None] - peer_pos[0][None, :]
    delta_y = own_pos[1][:, None] - peer_pos[1][None, :]
    delta_z = own_pos[2][:, None] - peer_pos[2][None, :]
    squared = delta_x * delta_x + delta_y * delta_y + delta_z * delta_z
    distance = jnp.sqrt(squared + 0.01)
    centers = jnp.arange(RBF, dtype=jnp.float32) * (cutoff / (RBF - 1))
    envelope = (1.0 - jnp.minimum(squared / (cutoff * cutoff), 1.0)) ** 2
    scaled = (distance[:, None, :] - centers[None, :, None]) / sigma_width
    return (jnp.exp(-scaled * scaled) * (envelope * mask_values)[:, None, :]).astype(jnp.bfloat16)

def reference(positions, features, block_counts, pair_list, pair_count, pair_mask, w_rbf, wavevectors, kfilter, w_in, w_out):
    atom_index = jnp.arange(ATOMS, dtype=jnp.int32)
    slab_of = atom_index // SLAB
    block_in_slab = atom_index % SLAB // BLOCK
    live_atoms = (block_in_slab < block_counts[slab_of]).astype(jnp.float32)
    channels = features.shape[1]

    def pair_step(carry, entry_index):
        device = entry_index // MAXP
        slot_index = entry_index % MAXP
        slab_index = device // N_NARROW
        narrow_index = device % N_NARROW
        local_block = pair_list[slab_index, narrow_index, 0, slot_index]
        offset = pair_list[slab_index, narrow_index, 1, slot_index]
        peer_block = pair_list[slab_index, narrow_index, 2, slot_index]
        taken = jnp.where(slot_index < pair_count[slab_index, narrow_index], 1.0, 0.0).astype(jnp.float32)
        own_start = ((slab_index * SLAB_BLOCKS + narrow_index * BLK_DEV + local_block) * BLOCK).astype(jnp.int32)
        peer_start = jnp.minimum(((slab_index + offset) * SLAB_BLOCKS + peer_block) * BLOCK, ATOMS - BLOCK).astype(jnp.int32)
        anchor = jnp.int32(0)
        own_pos = lax.dynamic_slice(positions, (anchor, own_start), (3, BLOCK))
        peer_pos = lax.dynamic_slice(positions, (anchor, peer_start), (3, BLOCK))
        own_feat = lax.dynamic_slice_in_dim(features, own_start, BLOCK, 0)
        peer_feat = lax.dynamic_slice_in_dim(features, peer_start, BLOCK, 0)
        mask_values = pair_mask[slab_index, narrow_index, slot_index].astype(jnp.float32)
        filters = radial_filters(own_pos, peer_pos, mask_values).astype(jnp.float32)
        own_terms = (own_feat[None] * w_rbf[:, None, :]).astype(jnp.bfloat16).astype(jnp.float32)
        peer_terms = (peer_feat[None] * w_rbf[:, None, :]).astype(jnp.bfloat16).astype(jnp.float32)
        to_own = jnp.einsum('akb,kbc->ac', filters, peer_terms)
        to_peer = jnp.einsum('akb,kac->bc', filters, own_terms)
        current = lax.dynamic_slice_in_dim(carry, own_start, BLOCK, 0)
        carry = lax.dynamic_update_slice_in_dim(carry, current + taken * to_own, own_start, 0)
        current = lax.dynamic_slice_in_dim(carry, peer_start, BLOCK, 0)
        carry = lax.dynamic_update_slice_in_dim(carry, current + taken * to_peer, peer_start, 0)
        return (carry, None)
    total_slots = N_WIDE * N_NARROW * MAXP
    short, _ = lax.scan(pair_step, jnp.zeros((ATOMS, channels), jnp.float32), jnp.arange(total_slots, dtype=jnp.int32))

    def slab_tables(slab_index):
        start = (slab_index * SLAB).astype(jnp.int32)
        slab_pos = lax.dynamic_slice_in_dim(positions, start, SLAB, 1)
        phases = wavevectors[0][:, None] * slab_pos[0][None, :] + wavevectors[1][:, None] * slab_pos[1][None, :] + wavevectors[2][:, None] * slab_pos[2][None, :]
        return (jnp.cos(phases).astype(jnp.bfloat16), jnp.sin(phases).astype(jnp.bfloat16), start)

    def factor_step(carry, slab_index):
        cosines, sines, start = slab_tables(slab_index)
        slab_feat = lax.dynamic_slice_in_dim(features, start, SLAB, 0)
        slab_live = lax.dynamic_slice_in_dim(live_atoms, start, SLAB, 0)
        weighted = (slab_feat * slab_live[:, None]).astype(jnp.bfloat16)
        return ((carry[0] + jnp.dot(cosines, weighted, preferred_element_type=jnp.float32), carry[1] + jnp.dot(sines, weighted, preferred_element_type=jnp.float32)), None)
    empty = jnp.zeros((K, channels), jnp.float32)
    slab_ids = jnp.arange(N_WIDE, dtype=jnp.int32)
    (struct_cos, struct_sin), _ = lax.scan(factor_step, (empty, empty), slab_ids)
    filt_cos = (kfilter * struct_cos / ATOMS).astype(jnp.bfloat16)
    filt_sin = (kfilter * struct_sin / ATOMS).astype(jnp.bfloat16)

    def long_slab(slab_index):
        cosines, sines, start = slab_tables(slab_index)
        return jnp.dot(cosines.T, filt_cos, preferred_element_type=jnp.float32) + jnp.dot(sines.T, filt_sin, preferred_element_type=jnp.float32)
    long_range = lax.map(long_slab, slab_ids).reshape(ATOMS, channels)
    message = (short + long_range).astype(jnp.bfloat16)
    hidden = jax.nn.silu(jnp.dot(message, w_in, preferred_element_type=jnp.float32)).astype(jnp.bfloat16)
    return live_atoms[:, None] * (features + jnp.dot(hidden, w_out, preferred_element_type=jnp.float32))
```

```python
import functools
import math

import jax
import jax.numpy as jnp
from jax import lax
from jax.experimental import pallas as pl
from jax.experimental.pallas import tpu as pltpu
from jax.sharding import PartitionSpec as P

cutoff = 2.0
sigma_width = 0.25
MESH = pl.DeviceIdType.MESH
f32, bf16 = jnp.float32, jnp.bfloat16

COS = (1.0, -19.73920440673828, 64.93911743164062, -85.45014190673828,
       60.167633056640625, -25.967601776123047, 6.528658866882324)
SIN = (6.2831854820251465, -41.34170150756836, 81.60513305664062, -76.70301818847656,
       42.02592849731445, -14.899847984313965, 3.238137722015381)


def horner(coefs, u):
    acc = coefs[-1]
    for c in coefs[-2::-1]:
        acc = acc * u + c
    return acc


def column(row, size):
    return jnp.transpose(jnp.broadcast_to(row, (size, size)))


def kernel(
    cfg,
    pos_ref, cnt_ref, list_ref, pcount_ref, wrbf_ref, wv_ref,
    feat_ref, mask_hbm, kf_hbm, win_hbm, wout_hbm,
    out_ref,
    both, bpos, table, table_t, fact, rbuf, gath, filt,
    gh, gt, yown, ypeer, tp, buf, own_acc, ncv, msg, msum, sb, fin,
    mask, kf, win, wout,
    lsem, psend, precv, fsend, frecv, nsend, nrecv, npsend, nprecv,
    asend, arecv, zsend, zrecv, msend, mrecv, esend, erecv,
):
    W, N, B, C, RBF, SLOTS = cfg
    w, n = lax.axis_index("wide"), lax.axis_index("narrow")
    bits = W.bit_length() - 1
    qdev = wv_ref.shape[1]
    rows = 2 * qdev

    locals_ = [
        pltpu.make_async_copy(feat_ref, both.at[n], lsem.at[0]),
        pltpu.make_async_copy(mask_hbm.at[0, 0], mask, lsem.at[1]),
        pltpu.make_async_copy(kf_hbm, kf, lsem.at[2]),
        pltpu.make_async_copy(win_hbm, win, lsem.at[3]),
        pltpu.make_async_copy(wout_hbm, wout, lsem.at[4]),
    ]
    for copy in locals_:
        copy.start()
    bpos[n] = pos_ref[...]

    barrier = pltpu.get_barrier_semaphore()
    partners = [dict(wide=w, narrow=lax.rem(n + d, N)) for d in range(1, N)]
    partners += [dict(wide=w + (1 - 2 * ((w // (1 << b)) % 2)) * (1 << b), narrow=n) for b in range(bits)]
    partners += [dict(wide=lax.rem(w + 1, W), narrow=n), dict(wide=lax.rem(w + W - 1, W), narrow=n)]
    for p in partners:
        pl.semaphore_signal(barrier, inc=1, device_id=p, device_id_type=MESH)
    pl.semaphore_wait(barrier, len(partners))

    def to(src, dst, ss, rs, **dev):
        ids = dict(wide=w, narrow=n)
        ids.update(dev)
        return pltpu.make_async_remote_copy(
            src_ref=src, dst_ref=dst, send_sem=ss, recv_sem=rs, device_id=ids, device_id_type=MESH
        )

    has_prev = w > 0
    has_next = w < W - 1
    prev = lax.rem(w + W - 1, W)
    nxt = lax.rem(w + 1, W)

    pos_out, feat_out = [], []
    for d in range(1, N):
        pos_out.append(to(pos_ref, bpos.at[n], psend.at[d], precv.at[d], narrow=lax.rem(n + d, N)))
        pos_out[-1].start()
    for d in (2, 1, 3) if N == 4 else range(1, N):
        feat_out.append(to(feat_ref, both.at[n], fsend.at[d], frecv.at[d], narrow=lax.rem(n + d, N)))
        feat_out[-1].start()

    def forward(i, j):
        return to(both.at[j], both.at[N + j], nsend.at[i], nrecv.at[i], wide=prev)

    locals_[0].wait()

    @pl.when(has_prev)
    def _():
        forward(0, n).start()

    for d in range(1, N):
        src = lax.rem(n + N - d, N)
        to(pos_ref, bpos.at[src], psend.at[d], precv.at[d], narrow=src).wait_recv()
    pos_fwd = to(bpos.at[pl.ds(0, N)], bpos.at[pl.ds(N, N)], npsend, nprecv, wide=prev)

    @pl.when(has_prev)
    def _():
        pos_fwd.start()

    def wave_chunk(qc, _):
        q0 = pl.multiple_of(qc * B, B)
        wc = [column(wv_ref[i : i + 1, pl.ds(q0, B)] * (0.5 / math.pi), B) for i in range(3)]

        def atom_chunk(j, _):
            p = bpos[j]
            t = wc[0] * p[0:1] + wc[1] * p[1:2] + wc[2] * p[2:3]
            t = t - jnp.round(t)
            u = t * t
            for base, value in ((0, horner(COS, u)), (qdev, t * horner(SIN, u))):
                at = pl.multiple_of(base + q0, B)
                table[pl.ds(at, B), pl.ds(pl.multiple_of(j * B, B), B)] = value.astype(bf16)
                table_t[j, :, pl.ds(at, B)] = jnp.transpose(value).astype(bf16)
            return 0

        return lax.fori_loop(0, N, atom_chunk, 0)

    lax.fori_loop(0, qdev // B, wave_chunk, 0)

    f_own = both[n]
    for k in range(RBF):
        yown[k * B : (k + 1) * B, :] = (f_own * wrbf_ref[k : k + 1, :]).astype(bf16)

    @pl.when(has_next)
    def _():
        to(bpos.at[pl.ds(0, N)], bpos.at[pl.ds(N, N)], npsend, nprecv, wide=prev).wait_recv()

    @pl.when(jnp.logical_not(has_next))
    def _():
        bpos[pl.ds(N, N)] = jnp.zeros((N,) + bpos.shape[1:], f32)

    locals_[1].wait()
    alpha = math.sqrt(math.log2(math.e)) / sigma_width
    for i in range(3):
        ncv[i] = column(pos_ref[i : i + 1, :], B)

    def slot_filters(s, _):
        p = bpos[list_ref[0, 0, 1, s] * N + list_ref[0, 0, 2, s]]
        taken = jnp.where(s < pcount_ref[0, 0], 1.0, 0.0).astype(f32)
        dx, dy, dz = ncv[0] - p[0:1], ncv[1] - p[1:2], ncv[2] - p[2:3]
        squared = dx * dx + dy * dy + dz * dz
        dist = jnp.sqrt(squared + 0.01) * alpha
        env = 1.0 - jnp.minimum(squared * (1.0 / (cutoff * cutoff)), 1.0)
        em = env * env * (mask[s].astype(f32) * taken)
        dist_t, em_t = jnp.transpose(dist), jnp.transpose(em)
        for k in range(RBF):
            center = k * (cutoff / (RBF - 1)) * alpha
            a = dist - center
            b = dist_t - center
            gh[s, :, k * B : (k + 1) * B] = (jnp.exp2(-(a * a)) * em).astype(bf16)
            gt[s, :, k * B : (k + 1) * B] = (jnp.exp2(-(b * b)) * em_t).astype(bf16)
        return 0

    lax.fori_loop(0, SLOTS, slot_filters, 0)

    for s in range(SLOTS):
        tp[s] = jnp.dot(gt[s], yown[...], preferred_element_type=f32)

    def spread(j, _):
        acc = jnp.zeros((B, C), f32)
        for s in range(SLOTS):
            hit = (list_ref[0, 0, 1, s] * N + list_ref[0, 0, 2, s]) == j
            acc = acc + tp[s] * jnp.where(hit, 1.0, 0.0).astype(f32)
        buf[j] = acc
        return 0

    lax.fori_loop(0, 2 * N, spread, 0)

    live = cnt_ref[0]

    def weight(j):
        return jnp.where(j < live, 1.0, 0.0).astype(f32)

    for i, d in enumerate((1, 2, 3) if N == 4 else range(1, N)):
        src = lax.rem(n + N - d, N)
        to(feat_ref, both.at[src], fsend.at[d], frecv.at[d], narrow=src).wait_recv()

        @pl.when(has_prev)
        def _():
            forward(d, src).start()

    weighted = jnp.concatenate([(both[j] * weight(j)).astype(bf16) for j in range(N)], axis=0)

    nh = 2 if (rows // 2) % (8 * W) == 0 else 1
    hrows = rows // nh
    orders = [list(range(bits)), [0] + list(range(bits - 1, 0, -1))][:nh]

    def bit_of(b):
        return (w // (1 << b)) % 2

    def partner(b):
        return w + (1 - 2 * bit_of(b)) * (1 << b)

    state = [dict(off=h * hrows, size=hrows, at=h * hrows) for h in range(nh)]
    pending = []

    def mult8(x):
        return pl.multiple_of(x, 8)

    def rs_start(h, s):
        st, b = state[h], orders[h][s]
        half = st["size"] // 2
        mine = st["off"] + bit_of(b) * half
        other = st["off"] + (1 - bit_of(b)) * half
        i = h * 2 * bits + s
        copy = to(fact.at[pl.ds(mult8(other), half)], rbuf.at[pl.ds(st["at"], half)], asend.at[i], arecv.at[i], wide=partner(b))
        copy.start()
        pending.append(copy)
        st.update(copy=copy, off=mine, size=half)

    def rs_finish(h, s):
        st = state[h]
        st["copy"].wait_recv()
        part = pl.ds(mult8(st["off"]), st["size"])
        total = fact[part, :] + rbuf[pl.ds(st["at"], st["size"]), :]
        st["at"] += st["size"]
        if s == bits - 1:
            gath[part, :] = total
        else:
            fact[part, :] = total

    def ag_start(h, s):
        st, b = state[h], orders[h][s]
        part = pl.ds(mult8(st["off"]), st["size"])
        i = h * 2 * bits + bits + s
        copy = to(gath.at[part], gath.at[part], asend.at[i], arecv.at[i], wide=partner(b))
        copy.start()
        pending.append(copy)

    def ag_finish(h, s):
        st, b = state[h], orders[h][s]
        i = h * 2 * bits + bits + s
        there = st["off"] + (1 - 2 * bit_of(b)) * st["size"]
        part = pl.ds(mult8(there), st["size"])
        to(gath.at[part], gath.at[part], asend.at[i], arecv.at[i], wide=partner(b)).wait_recv()
        st.update(off=st["off"] - bit_of(b) * st["size"], size=st["size"] * 2)

    step = min(hrows, 256)
    for h in range(nh):
        for r in range(h * hrows, (h + 1) * hrows, step):
            fact[r : r + step, :] = jnp.dot(table[r : r + step, :], weighted, preferred_element_type=f32)
        rs_start(h, 0)

    znext = []
    for d in range(1, N):
        j = lax.rem(n + d, N)
        znext.append(to(buf.at[N + j], sb.at[d], zsend.at[d], zrecv.at[d], narrow=j))
        znext[-1].start()

    def job_peer(s):
        def run():
            if s == 0:
                for i in range(N):
                    j = lax.rem(n + N - i, N)

                    @pl.when(has_next)
                    def _():
                        forward(i, j).wait_recv()

                @pl.when(jnp.logical_not(has_next))
                def _():
                    for i in range(N):
                        both[N + i] = jnp.zeros((B, C), f32)

            f_peer = both[list_ref[0, 0, 1, s] * N + list_ref[0, 0, 2, s]]
            for k in range(RBF):
                ypeer[k * B : (k + 1) * B, :] = (f_peer * wrbf_ref[k : k + 1, :]).astype(bf16)
            value = jnp.dot(gh[s], ypeer[...], preferred_element_type=f32)
            own_acc[...] = value if s == 0 else own_acc[...] + value

        return run

    def job_next():
        for copy in znext:
            copy.wait_recv()
        msum[...] = buf[N + n] + sb[1] + sb[2] + sb[3] if N == 4 else sum((sb[d] for d in range(1, N)), buf[N + n])

        @pl.when(has_next)
        def _():
            to(msum, msg, msend, mrecv, wide=nxt).start()

    jobs = [job_peer(s) for s in range(SLOTS)]
    jobs.insert(min(2, len(jobs)), job_next)
    for s in range(2 * bits):
        if jobs:
            jobs.pop(0)()
        for h in range(nh):
            if s < bits:
                rs_finish(h, s)
                if s < bits - 1:
                    rs_start(h, s + 1)
                else:
                    ag_start(h, bits - 1)
            else:
                a = 2 * bits - 1 - s
                ag_finish(h, a)
                if a > 0:
                    ag_start(h, a - 1)
    for job in jobs:
        job()

    atoms_all = B * N * W
    locals_[2].wait()
    for base in (0, qdev):
        filt[base : base + qdev, :] = (kf[...] * gath[base : base + qdev, :] / atoms_all).astype(bf16)

    last = []
    for d in (2, 1, 3) if N == 4 else range(1, N):
        j = lax.rem(n + d, N)
        fin[d] = buf[j] + jnp.dot(table_t[j], filt[...], preferred_element_type=f32)
        last.append(to(fin.at[d], fin.at[N + d], esend.at[d], erecv.at[d], narrow=j))
        last[-1].start()
    own = buf[n] + own_acc[...] + jnp.dot(table_t[n], filt[...], preferred_element_type=f32)

    @pl.when(has_prev)
    def _():
        to(msum, msg, msend, mrecv, wide=nxt).wait_recv()

    @pl.when(jnp.logical_not(has_prev))
    def _():
        msg[...] = jnp.zeros_like(msg)

    own = own + msg[...]
    locals_[3].wait()
    locals_[4].wait()
    for copy in last:
        copy.wait_recv()
    for d in range(1, N):
        own = own + fin[N + d]
    hidden = jnp.dot(own.astype(bf16), win[...], preferred_element_type=f32)
    hidden = (hidden / (1.0 + jnp.exp(-hidden))).astype(bf16)
    out_ref[...] = weight(n) * (both[n] + jnp.dot(hidden, wout[...], preferred_element_type=f32))

    for copy in pos_out + feat_out + znext + last + pending:
        copy.wait_send()

    @pl.when(has_prev)
    def _():
        pos_fwd.wait_send()
        for i in range(N):
            forward(i, lax.rem(n + N - i, N)).wait_send()

    @pl.when(has_next)
    def _():
        to(msum, msg, msend, mrecv, wide=nxt).wait_send()


def local(W, N, positions, features, block_counts, pair_list, pair_count, pair_mask, w_rbf, wavevectors, kfilter, w_in, w_out):
    B, C = features.shape
    RBF = w_rbf.shape[0]
    SLOTS = pair_list.shape[3]
    rows = 2 * wavevectors.shape[1]
    bits = W.bit_length() - 1
    vmem = pl.BlockSpec(memory_space=pltpu.VMEM)
    smem = pl.BlockSpec(memory_space=pltpu.SMEM)
    hbm = pl.BlockSpec(memory_space=pl.ANY)
    dma = pltpu.SemaphoreType.DMA
    V = pltpu.VMEM
    return pl.pallas_call(
        functools.partial(kernel, (W, N, B, C, RBF, SLOTS)),
        out_shape=jax.ShapeDtypeStruct((B, C), f32),
        in_specs=[vmem, smem, smem, smem, vmem, vmem, hbm, hbm, hbm, hbm, hbm],
        out_specs=vmem,
        scratch_shapes=[
            V((2 * N, B, C), f32),
            V((2 * N, 3, B), f32),
            V((rows, N * B), bf16),
            V((N, B, rows), bf16),
            V((rows, C), f32),
            V((rows, C), f32),
            V((rows, C), f32),
            V((rows, C), bf16),
            V((SLOTS, B, RBF * B), bf16),
            V((SLOTS, B, RBF * B), bf16),
            V((RBF * B, C), bf16),
            V((RBF * B, C), bf16),
            V((SLOTS, B, C), f32),
            V((2 * N, B, C), f32),
            V((B, C), f32),
            V((3, B, B), f32),
            V((B, C), f32),
            V((B, C), f32),
            V((N, B, C), f32),
            V((2 * N, B, C), f32),
            V(pair_mask.shape[2:], jnp.int32),
            V(kfilter.shape, f32),
            V(w_in.shape, bf16),
            V(w_out.shape, bf16),
            dma((5,)),
            dma((N,)), dma((N,)),
            dma((N,)), dma((N,)),
            dma((N,)), dma((N,)),
            dma, dma,
            dma((4 * bits,)), dma((4 * bits,)),
            dma((N,)), dma((N,)),
            dma, dma,
            dma((N,)), dma((N,)),
        ],
        compiler_params=pltpu.CompilerParams(
            collective_id=0, has_side_effects=True, vmem_limit_bytes=48 << 20
        ),
    )(positions, block_counts, pair_list, pair_count, w_rbf, wavevectors, features, pair_mask, kfilter, w_in, w_out)


def solution(mesh):
    placed = (
        P(None, ("wide", "narrow")),
        P(("wide", "narrow"), None),
        P("wide"),
        P("wide", "narrow", None, None),
        P("wide", "narrow"),
        P("wide", "narrow", None, None, None),
        P(),
        P(None, "narrow"),
        P("narrow", None),
        P(),
        P(),
    )
    body = functools.partial(local, mesh.shape["wide"], mesh.shape["narrow"])
    return jax.shard_map(
        body, mesh=mesh, in_specs=placed, out_specs=P(("wide", "narrow"), None), check_vma=False
    )
```

```python
import functools
import math

import jax
import jax.numpy as jnp
from jax import lax
from jax.experimental import pallas as pl
from jax.experimental.pallas import tpu as pltpu
from jax.sharding import PartitionSpec as P

cutoff = 2.0
sigma_width = 0.25
MESH = pl.DeviceIdType.MESH
f32, bf16 = jnp.float32, jnp.bfloat16

COS = (1.0, -19.73920440673828, 64.93911743164062, -85.45014190673828,
       60.167633056640625, -25.967601776123047, 6.528658866882324)
SIN = (6.2831854820251465, -41.34170150756836, 81.60513305664062, -76.70301818847656,
       42.02592849731445, -14.899847984313965, 3.238137722015381)


def horner(coefs, u):
    acc = coefs[-1]
    for c in coefs[-2::-1]:
        acc = acc * u + c
    return acc


def column(row, size):
    return jnp.transpose(jnp.broadcast_to(row, (size, size)))


def kernel(
    cfg,
    cnt_ref, list_ref, pcount_ref,
    pos_hbm, wrbf_hbm, wv_hbm, feat_ref, mask_hbm, kf_hbm, win_hbm, wout_hbm,
    out_ref,
    pos_ref, wrbf_ref, wv_ref,
    both, bpos, table, table_t, fact, rbuf, gath, filt,
    gh, gt, yown, ypeer, tp, buf, own_acc, ncv, msg, msum, sb, fin,
    mask, kf, win, wout,
    lsem, psend, precv, fsend, frecv, nsend, nrecv, npsend, nprecv,
    asend, arecv, zsend, zrecv, msend, mrecv, esend, erecv,
):
    W, N, B, C, RBF, SLOTS = cfg
    w, n = lax.axis_index("wide"), lax.axis_index("narrow")
    bits = W.bit_length() - 1
    qdev = wv_ref.shape[1]
    rows = 2 * qdev

    locals_ = [
        pltpu.make_async_copy(feat_ref, both.at[n], lsem.at[0]),
        pltpu.make_async_copy(mask_hbm.at[0, 0], mask, lsem.at[1]),
        pltpu.make_async_copy(kf_hbm, kf, lsem.at[2]),
        pltpu.make_async_copy(win_hbm, win, lsem.at[3]),
        pltpu.make_async_copy(wout_hbm, wout, lsem.at[4]),
        pltpu.make_async_copy(pos_hbm, pos_ref, lsem.at[5]),
        pltpu.make_async_copy(wrbf_hbm, wrbf_ref, lsem.at[6]),
        pltpu.make_async_copy(wv_hbm, wv_ref, lsem.at[7]),
        pltpu.make_async_copy(pos_hbm, bpos.at[n], lsem.at[8]),
    ]
    for i in (5, 8, 7, 0, 6, 1, 2, 3, 4):
        locals_[i].start()

    barrier = pltpu.get_barrier_semaphore()
    partners = [dict(wide=w, narrow=lax.rem(n + d, N)) for d in range(1, N)]
    partners += [dict(wide=w + (1 - 2 * ((w // (1 << b)) % 2)) * (1 << b), narrow=n) for b in range(bits)]
    partners += [dict(wide=lax.rem(w + 1, W), narrow=n), dict(wide=lax.rem(w + W - 1, W), narrow=n)]
    for p in partners:
        pl.semaphore_signal(barrier, inc=1, device_id=p, device_id_type=MESH)
    pl.semaphore_wait(barrier, len(partners))

    def to(src, dst, ss, rs, **dev):
        ids = dict(wide=w, narrow=n)
        ids.update(dev)
        return pltpu.make_async_remote_copy(
            src_ref=src, dst_ref=dst, send_sem=ss, recv_sem=rs, device_id=ids, device_id_type=MESH
        )

    has_prev = w > 0
    has_next = w < W - 1
    prev = lax.rem(w + W - 1, W)
    nxt = lax.rem(w + 1, W)

    pos_out, feat_out = [], []
    for d in range(1, N):
        pos_out.append(to(pos_hbm, bpos.at[n], psend.at[d], precv.at[d], narrow=lax.rem(n + d, N)))
        pos_out[-1].start()
    for d in (2, 1, 3) if N == 4 else range(1, N):
        feat_out.append(to(feat_ref, both.at[n], fsend.at[d], frecv.at[d], narrow=lax.rem(n + d, N)))
        feat_out[-1].start()

    def forward(i, j):
        return to(both.at[j], both.at[N + j], nsend.at[i], nrecv.at[i], wide=prev)

    for i in (0, 5, 6, 7, 8):
        locals_[i].wait()

    @pl.when(has_prev)
    def _():
        forward(0, n).start()

    for d in range(1, N):
        src = lax.rem(n + N - d, N)
        to(pos_ref, bpos.at[src], psend.at[d], precv.at[d], narrow=src).wait_recv()
    pos_fwd = to(bpos.at[pl.ds(0, N)], bpos.at[pl.ds(N, N)], npsend, nprecv, wide=prev)

    @pl.when(has_prev)
    def _():
        pos_fwd.start()

    def wave_chunk(qc, _):
        q0 = pl.multiple_of(qc * B, B)
        wc = [column(wv_ref[i : i + 1, pl.ds(q0, B)] * (0.5 / math.pi), B) for i in range(3)]

        def atom_chunk(j, _):
            p = bpos[j]
            t = wc[0] * p[0:1] + wc[1] * p[1:2] + wc[2] * p[2:3]
            t = t - jnp.round(t)
            u = t * t
            for base, value in ((0, horner(COS, u)), (qdev, t * horner(SIN, u))):
                at = pl.multiple_of(base + q0, B)
                table[pl.ds(at, B), pl.ds(pl.multiple_of(j * B, B), B)] = value.astype(bf16)
                table_t[j, :, pl.ds(at, B)] = jnp.transpose(value).astype(bf16)
            return 0

        return lax.fori_loop(0, N, atom_chunk, 0)

    lax.fori_loop(0, qdev // B, wave_chunk, 0)

    f_own = both[n]
    for k in range(RBF):
        yown[k * B : (k + 1) * B, :] = (f_own * wrbf_ref[k : k + 1, :]).astype(bf16)

    @pl.when(has_next)
    def _():
        to(bpos.at[pl.ds(0, N)], bpos.at[pl.ds(N, N)], npsend, nprecv, wide=prev).wait_recv()

    @pl.when(jnp.logical_not(has_next))
    def _():
        bpos[pl.ds(N, N)] = jnp.zeros((N,) + bpos.shape[1:], f32)

    locals_[1].wait()
    alpha = math.sqrt(math.log2(math.e)) / sigma_width
    for i in range(3):
        ncv[i] = column(pos_ref[i : i + 1, :], B)

    def slot_filters(s, _):
        p = bpos[list_ref[0, 1, 0, s] * N + list_ref[0, 2, 0, s]]
        taken = jnp.where(s < pcount_ref[0, 0], 1.0, 0.0).astype(f32)
        dx, dy, dz = ncv[0] - p[0:1], ncv[1] - p[1:2], ncv[2] - p[2:3]
        squared = dx * dx + dy * dy + dz * dz
        dist = jnp.sqrt(squared + 0.01) * alpha
        env = 1.0 - jnp.minimum(squared * (1.0 / (cutoff * cutoff)), 1.0)
        em = env * env * (mask[s].astype(f32) * taken)
        dist_t, em_t = jnp.transpose(dist), jnp.transpose(em)
        for k in range(RBF):
            center = k * (cutoff / (RBF - 1)) * alpha
            a = dist - center
            b = dist_t - center
            gh[s, :, k * B : (k + 1) * B] = (jnp.exp2(-(a * a)) * em).astype(bf16)
            gt[s, :, k * B : (k + 1) * B] = (jnp.exp2(-(b * b)) * em_t).astype(bf16)
        return 0

    lax.fori_loop(0, SLOTS, slot_filters, 0)

    for s in range(SLOTS):
        tp[s] = jnp.dot(gt[s], yown[...], preferred_element_type=f32)

    def spread(j, _):
        acc = jnp.zeros((B, C), f32)
        for s in range(SLOTS):
            hit = (list_ref[0, 1, 0, s] * N + list_ref[0, 2, 0, s]) == j
            acc = acc + tp[s] * jnp.where(hit, 1.0, 0.0).astype(f32)
        buf[j] = acc
        return 0

    lax.fori_loop(0, 2 * N, spread, 0)

    live = cnt_ref[0]

    def weight(j):
        return jnp.where(j < live, 1.0, 0.0).astype(f32)

    for i, d in enumerate((1, 2, 3) if N == 4 else range(1, N)):
        src = lax.rem(n + N - d, N)
        to(feat_ref, both.at[src], fsend.at[d], frecv.at[d], narrow=src).wait_recv()

        @pl.when(has_prev)
        def _():
            forward(d, src).start()

    weighted = jnp.concatenate([(both[j] * weight(j)).astype(bf16) for j in range(N)], axis=0)

    nh = 2 if (rows // 2) % (8 * W) == 0 else 1
    hrows = rows // nh
    orders = [list(range(bits)), [0] + list(range(bits - 1, 0, -1))][:nh]

    def bit_of(b):
        return (w // (1 << b)) % 2

    def partner(b):
        return w + (1 - 2 * bit_of(b)) * (1 << b)

    state = [dict(off=h * hrows, size=hrows, at=h * hrows) for h in range(nh)]
    pending = []

    def mult8(x):
        return pl.multiple_of(x, 8)

    def rs_start(h, s):
        st, b = state[h], orders[h][s]
        half = st["size"] // 2
        mine = st["off"] + bit_of(b) * half
        other = st["off"] + (1 - bit_of(b)) * half
        i = h * 2 * bits + s
        copy = to(fact.at[pl.ds(mult8(other), half)], rbuf.at[pl.ds(st["at"], half)], asend.at[i], arecv.at[i], wide=partner(b))
        copy.start()
        pending.append(copy)
        st.update(copy=copy, off=mine, size=half)

    def rs_finish(h, s):
        st = state[h]
        st["copy"].wait_recv()
        part = pl.ds(mult8(st["off"]), st["size"])
        total = fact[part, :] + rbuf[pl.ds(st["at"], st["size"]), :]
        st["at"] += st["size"]
        if s == bits - 1:
            gath[part, :] = total
        else:
            fact[part, :] = total

    def ag_start(h, s):
        st, b = state[h], orders[h][s]
        part = pl.ds(mult8(st["off"]), st["size"])
        i = h * 2 * bits + bits + s
        copy = to(gath.at[part], gath.at[part], asend.at[i], arecv.at[i], wide=partner(b))
        copy.start()
        pending.append(copy)

    def ag_finish(h, s):
        st, b = state[h], orders[h][s]
        i = h * 2 * bits + bits + s
        there = st["off"] + (1 - 2 * bit_of(b)) * st["size"]
        part = pl.ds(mult8(there), st["size"])
        to(gath.at[part], gath.at[part], asend.at[i], arecv.at[i], wide=partner(b)).wait_recv()
        st.update(off=st["off"] - bit_of(b) * st["size"], size=st["size"] * 2)

    step = min(hrows, 256)
    for h in range(nh):
        for r in range(h * hrows, (h + 1) * hrows, step):
            fact[r : r + step, :] = jnp.dot(table[r : r + step, :], weighted, preferred_element_type=f32)
        rs_start(h, 0)

    znext = []
    for d in range(1, N):
        j = lax.rem(n + d, N)
        znext.append(to(buf.at[N + j], sb.at[d], zsend.at[d], zrecv.at[d], narrow=j))
        znext[-1].start()

    def job_peer(s):
        def run():
            if s == 0:
                for i in range(N):
                    j = lax.rem(n + N - i, N)

                    @pl.when(has_next)
                    def _():
                        forward(i, j).wait_recv()

                @pl.when(jnp.logical_not(has_next))
                def _():
                    for i in range(N):
                        both[N + i] = jnp.zeros((B, C), f32)

            f_peer = both[list_ref[0, 1, 0, s] * N + list_ref[0, 2, 0, s]]
            for k in range(RBF):
                ypeer[k * B : (k + 1) * B, :] = (f_peer * wrbf_ref[k : k + 1, :]).astype(bf16)
            value = jnp.dot(gh[s], ypeer[...], preferred_element_type=f32)
            own_acc[...] = value if s == 0 else own_acc[...] + value

        return run

    def job_next():
        for copy in znext:
            copy.wait_recv()
        msum[...] = buf[N + n] + sb[1] + sb[2] + sb[3] if N == 4 else sum((sb[d] for d in range(1, N)), buf[N + n])

        @pl.when(has_next)
        def _():
            to(msum, msg, msend, mrecv, wide=nxt).start()

    jobs = [job_peer(s) for s in range(SLOTS)]
    jobs.insert(min(2, len(jobs)), job_next)
    for s in range(2 * bits):
        if jobs:
            jobs.pop(0)()
        for h in range(nh):
            if s < bits:
                rs_finish(h, s)
                if s < bits - 1:
                    rs_start(h, s + 1)
                else:
                    ag_start(h, bits - 1)
            else:
                a = 2 * bits - 1 - s
                ag_finish(h, a)
                if a > 0:
                    ag_start(h, a - 1)
    for job in jobs:
        job()

    atoms_all = B * N * W
    locals_[2].wait()
    for base in (0, qdev):
        filt[base : base + qdev, :] = (kf[...] * gath[base : base + qdev, :] / atoms_all).astype(bf16)

    last = []
    for d in (2, 1, 3) if N == 4 else range(1, N):
        j = lax.rem(n + d, N)
        fin[d] = buf[j] + jnp.dot(table_t[j], filt[...], preferred_element_type=f32)
        last.append(to(fin.at[d], fin.at[N + d], esend.at[d], erecv.at[d], narrow=j))
        last[-1].start()
    own = buf[n] + own_acc[...] + jnp.dot(table_t[n], filt[...], preferred_element_type=f32)

    @pl.when(has_prev)
    def _():
        to(msum, msg, msend, mrecv, wide=nxt).wait_recv()

    @pl.when(jnp.logical_not(has_prev))
    def _():
        msg[...] = jnp.zeros_like(msg)

    own = own + msg[...]
    locals_[3].wait()
    locals_[4].wait()
    for copy in last:
        copy.wait_recv()
    for d in range(1, N):
        own = own + fin[N + d]
    hidden = jnp.dot(own.astype(bf16), win[...], preferred_element_type=f32)
    hidden = (hidden / (1.0 + jnp.exp(-hidden))).astype(bf16)
    out_ref[...] = weight(n) * (both[n] + jnp.dot(hidden, wout[...], preferred_element_type=f32))

    for copy in pos_out + feat_out + znext + last + pending:
        copy.wait_send()

    @pl.when(has_prev)
    def _():
        pos_fwd.wait_send()
        for i in range(N):
            forward(i, lax.rem(n + N - i, N)).wait_send()

    @pl.when(has_next)
    def _():
        to(msum, msg, msend, mrecv, wide=nxt).wait_send()


def local(W, N, positions, features, block_counts, pair_list, pair_count, pair_mask, w_rbf, wavevectors, kfilter, w_in, w_out):
    B, C = features.shape
    RBF = w_rbf.shape[0]
    SLOTS = pair_list.shape[3]
    rows = 2 * wavevectors.shape[1]
    bits = W.bit_length() - 1
    vmem = pl.BlockSpec(memory_space=pltpu.VMEM)
    smem = pl.BlockSpec(memory_space=pltpu.SMEM)
    hbm = pl.BlockSpec(memory_space=pltpu.HBM)
    dma = pltpu.SemaphoreType.DMA
    V = pltpu.VMEM
    return pl.pallas_call(
        functools.partial(kernel, (W, N, B, C, RBF, SLOTS)),
        out_shape=jax.ShapeDtypeStruct((B, C), f32),
        in_specs=[smem] * 3 + [hbm] * 8,
        out_specs=vmem,
        scratch_shapes=[
            V(positions.shape, f32),
            V(w_rbf.shape, f32),
            V(wavevectors.shape, f32),
            V((2 * N, B, C), f32),
            V((2 * N, 3, B), f32),
            V((rows, N * B), bf16),
            V((N, B, rows), bf16),
            V((rows, C), f32),
            V((rows, C), f32),
            V((rows, C), f32),
            V((rows, C), bf16),
            V((SLOTS, B, RBF * B), bf16),
            V((SLOTS, B, RBF * B), bf16),
            V((RBF * B, C), bf16),
            V((RBF * B, C), bf16),
            V((SLOTS, B, C), f32),
            V((2 * N, B, C), f32),
            V((B, C), f32),
            V((3, B, B), f32),
            V((B, C), f32),
            V((B, C), f32),
            V((N, B, C), f32),
            V((2 * N, B, C), f32),
            V(pair_mask.shape[2:], jnp.int32),
            V(kfilter.shape, f32),
            V(w_in.shape, bf16),
            V(w_out.shape, bf16),
            dma((9,)),
            dma((N,)), dma((N,)),
            dma((N,)), dma((N,)),
            dma((N,)), dma((N,)),
            dma, dma,
            dma((4 * bits,)), dma((4 * bits,)),
            dma((N,)), dma((N,)),
            dma, dma,
            dma((N,)), dma((N,)),
        ],
        compiler_params=pltpu.CompilerParams(
            collective_id=0, has_side_effects=True, vmem_limit_bytes=67043328
        ),
    )(block_counts, jnp.transpose(pair_list, (0, 2, 1, 3)), pair_count, positions, w_rbf, wavevectors, features, pair_mask, kfilter, w_in, w_out)


def solution(mesh):
    placed = (
        P(None, ("wide", "narrow")),
        P(("wide", "narrow"), None),
        P("wide"),
        P("wide", "narrow", None, None),
        P("wide", "narrow"),
        P("wide", "narrow", None, None, None),
        P(),
        P(None, "narrow"),
        P("narrow", None),
        P(),
        P(),
    )
    body = functools.partial(local, mesh.shape["wide"], mesh.shape["narrow"])
    return jax.shard_map(
        body, mesh=mesh, in_specs=placed, out_specs=P(("wide", "narrow"), None), check_vma=False
    )
```

```python
import functools
import math

import jax
import jax.numpy as jnp
from jax import lax
from jax.experimental import pallas as pl
from jax.experimental.pallas import tpu as pltpu
from jax.sharding import PartitionSpec as P

cutoff = 2.0
sigma_width = 0.25
MESH = pl.DeviceIdType.MESH
CHAINS = (8, 4, 2, 1)
f32, bf16 = jnp.float32, jnp.bfloat16

COS = (1.0, -19.73920440673828, 64.93911743164062, -85.45014190673828,
       60.167633056640625, -25.967601776123047, 6.528658866882324)
SIN = (6.2831854820251465, -41.34170150756836, 81.60513305664062, -76.70301818847656,
       42.02592849731445, -14.899847984313965, 3.238137722015381)


def horner(coefs, u):
    acc = coefs[-1]
    for c in coefs[-2::-1]:
        acc = acc * u + c
    return acc


def column(row, size):
    return jnp.transpose(jnp.broadcast_to(row, (size, size)))


def kernel(
    cfg,
    cnt_ref, list_ref, pcount_ref,
    pos_hbm, wrbf_hbm, wv_hbm, feat_ref, mask_hbm, kf_hbm, win_hbm, wout_hbm,
    out_ref,
    pos_ref, wrbf_ref, wv_ref,
    both, bpos, table, table_t, fact, rbuf, gath, filt,
    gh, gt, yown, ypeer, tp, buf, own_acc, ncv, msg, msum, sb, fin,
    mask, kf, win, wout,
    lsem, psend, precv, fsend, frecv, nsend, nrecv, npsend, nprecv,
    asend, arecv, zsend, zrecv, msend, mrecv, esend, erecv,
):
    W, N, B, C, RBF, SLOTS = cfg
    w, n = lax.axis_index("wide"), lax.axis_index("narrow")
    bits = W.bit_length() - 1
    qdev = wv_ref.shape[1]
    rows = 2 * qdev

    locals_ = [
        pltpu.make_async_copy(feat_ref, both.at[n], lsem.at[0]),
        pltpu.make_async_copy(mask_hbm.at[0, 0], mask, lsem.at[1]),
        pltpu.make_async_copy(kf_hbm, kf, lsem.at[2]),
        pltpu.make_async_copy(win_hbm, win, lsem.at[3]),
        pltpu.make_async_copy(wout_hbm, wout, lsem.at[4]),
        pltpu.make_async_copy(pos_hbm, pos_ref, lsem.at[5]),
        pltpu.make_async_copy(wrbf_hbm, wrbf_ref, lsem.at[6]),
        pltpu.make_async_copy(wv_hbm, wv_ref, lsem.at[7]),
        pltpu.make_async_copy(pos_hbm, bpos.at[n], lsem.at[8]),
    ]
    for i in (5, 8, 7, 0, 6, 1, 2, 3, 4):
        locals_[i].start()

    barrier = pltpu.get_barrier_semaphore()
    partners = [dict(wide=w, narrow=lax.rem(n + d, N)) for d in range(1, N)]
    partners += [dict(wide=w + (1 - 2 * ((w // (1 << b)) % 2)) * (1 << b), narrow=n) for b in range(bits)]
    partners += [dict(wide=lax.rem(w + 1, W), narrow=n), dict(wide=lax.rem(w + W - 1, W), narrow=n)]
    for p in partners:
        pl.semaphore_signal(barrier, inc=1, device_id=p, device_id_type=MESH)
    pl.semaphore_wait(barrier, len(partners))

    def to(src, dst, ss, rs, **dev):
        ids = dict(wide=w, narrow=n)
        ids.update(dev)
        return pltpu.make_async_remote_copy(
            src_ref=src, dst_ref=dst, send_sem=ss, recv_sem=rs, device_id=ids, device_id_type=MESH
        )

    has_prev = w > 0
    has_next = w < W - 1
    prev = lax.rem(w + W - 1, W)
    nxt = lax.rem(w + 1, W)

    pos_out, feat_out = [], []
    for d in range(1, N):
        pos_out.append(to(pos_hbm, bpos.at[n], psend.at[d], precv.at[d], narrow=lax.rem(n + d, N)))
        pos_out[-1].start()
    for d in (2, 1, 3) if N == 4 else range(1, N):
        feat_out.append(to(feat_ref, both.at[n], fsend.at[d], frecv.at[d], narrow=lax.rem(n + d, N)))
        feat_out[-1].start()

    def forward(i, j):
        return to(both.at[j], both.at[N + j], nsend.at[i], nrecv.at[i], wide=prev)

    for i in (0, 5, 6, 7, 8):
        locals_[i].wait()

    @pl.when(has_prev)
    def _():
        forward(0, n).start()

    for d in range(1, N):
        src = lax.rem(n + N - d, N)
        to(pos_ref, bpos.at[src], psend.at[d], precv.at[d], narrow=src).wait_recv()
    pos_fwd = to(bpos.at[pl.ds(0, N)], bpos.at[pl.ds(N, N)], npsend, nprecv, wide=prev)

    @pl.when(has_prev)
    def _():
        pos_fwd.start()

    def wave_chunk(qc, _):
        q0 = pl.multiple_of(qc * B, B)
        wc = [column(wv_ref[i : i + 1, pl.ds(q0, B)] * (0.5 / math.pi), B) for i in range(3)]

        def atom_chunk(j, _):
            p = bpos[j]
            t = wc[0] * p[0:1] + wc[1] * p[1:2] + wc[2] * p[2:3]
            t = t - jnp.round(t)
            u = t * t
            for base, value in ((0, horner(COS, u)), (qdev, t * horner(SIN, u))):
                at = pl.multiple_of(base + q0, B)
                table[pl.ds(at, B), pl.ds(pl.multiple_of(j * B, B), B)] = value.astype(bf16)
                table_t[j, :, pl.ds(at, B)] = jnp.transpose(value).astype(bf16)
            return 0

        return lax.fori_loop(0, N, atom_chunk, 0)

    lax.fori_loop(0, qdev // B, wave_chunk, 0)

    f_own = both[n]
    for k in range(RBF):
        yown[k * B : (k + 1) * B, :] = (f_own * wrbf_ref[k : k + 1, :]).astype(bf16)

    @pl.when(has_next)
    def _():
        to(bpos.at[pl.ds(0, N)], bpos.at[pl.ds(N, N)], npsend, nprecv, wide=prev).wait_recv()

    @pl.when(jnp.logical_not(has_next))
    def _():
        bpos[pl.ds(N, N)] = jnp.zeros((N,) + bpos.shape[1:], f32)

    locals_[1].wait()
    alpha = math.sqrt(math.log2(math.e)) / sigma_width
    for i in range(3):
        ncv[i] = column(pos_ref[i : i + 1, :], B)

    def slot_filters(s, _):
        p = bpos[list_ref[0, 1, 0, s] * N + list_ref[0, 2, 0, s]]
        taken = jnp.where(s < pcount_ref[0, 0], 1.0, 0.0).astype(f32)
        dx, dy, dz = ncv[0] - p[0:1], ncv[1] - p[1:2], ncv[2] - p[2:3]
        squared = dx * dx + dy * dy + dz * dz
        dist = jnp.sqrt(squared + 0.01) * alpha
        env = 1.0 - jnp.minimum(squared * (1.0 / (cutoff * cutoff)), 1.0)
        em = env * env * (mask[s].astype(f32) * taken)
        dist_t, em_t = jnp.transpose(dist), jnp.transpose(em)
        for k in range(RBF):
            center = k * (cutoff / (RBF - 1)) * alpha
            a = dist - center
            b = dist_t - center
            gh[s, :, k * B : (k + 1) * B] = (jnp.exp2(-(a * a)) * em).astype(bf16)
            gt[s, :, k * B : (k + 1) * B] = (jnp.exp2(-(b * b)) * em_t).astype(bf16)
        return 0

    lax.fori_loop(0, SLOTS, slot_filters, 0)

    for s in range(SLOTS):
        tp[s] = jnp.dot(gt[s], yown[...], preferred_element_type=f32)

    def spread(j, _):
        acc = jnp.zeros((B, C), f32)
        for s in range(SLOTS):
            hit = (list_ref[0, 1, 0, s] * N + list_ref[0, 2, 0, s]) == j
            acc = acc + tp[s] * jnp.where(hit, 1.0, 0.0).astype(f32)
        buf[j] = acc
        return 0

    lax.fori_loop(0, 2 * N, spread, 0)

    znext = []
    for d in range(1, N):
        j = lax.rem(n + d, N)
        znext.append(to(buf.at[N + j], sb.at[d], zsend.at[d], zrecv.at[d], narrow=j))
        znext[-1].start()

    live = cnt_ref[0]

    def weight(j):
        return jnp.where(j < live, 1.0, 0.0).astype(f32)

    for i, d in enumerate((1, 2, 3) if N == 4 else range(1, N)):
        src = lax.rem(n + N - d, N)
        to(feat_ref, both.at[src], fsend.at[d], frecv.at[d], narrow=src).wait_recv()

        @pl.when(has_prev)
        def _():
            forward(d, src).start()

    weighted = jnp.concatenate([(both[j] * weight(j)).astype(bf16) for j in range(N)], axis=0)

    nh = next(c for c in CHAINS if rows % (c * 8 * W) == 0)
    hrows = rows // nh
    orders = [list(range(bits)) if h % 2 == 0 else [0] + list(range(bits - 1, 0, -1)) for h in range(nh)]

    def bit_of(b):
        return (w // (1 << b)) % 2

    def partner(b):
        return w + (1 - 2 * bit_of(b)) * (1 << b)

    state = [dict(off=h * hrows, size=hrows, at=h * hrows) for h in range(nh)]
    pending = []

    def mult8(x):
        return pl.multiple_of(x, 8)

    def rs_start(h, s):
        st, b = state[h], orders[h][s]
        half = st["size"] // 2
        mine = st["off"] + bit_of(b) * half
        other = st["off"] + (1 - bit_of(b)) * half
        i = h * 2 * bits + s
        copy = to(fact.at[pl.ds(mult8(other), half)], rbuf.at[pl.ds(st["at"], half)], asend.at[i], arecv.at[i], wide=partner(b))
        copy.start()
        pending.append(copy)
        st.update(copy=copy, off=mine, size=half)

    def rs_finish(h, s):
        st = state[h]
        st["copy"].wait_recv()
        part = pl.ds(mult8(st["off"]), st["size"])
        total = fact[part, :] + rbuf[pl.ds(st["at"], st["size"]), :]
        st["at"] += st["size"]
        if s == bits - 1:
            gath[part, :] = total
        else:
            fact[part, :] = total

    def ag_start(h, s):
        st, b = state[h], orders[h][s]
        part = pl.ds(mult8(st["off"]), st["size"])
        i = h * 2 * bits + bits + s
        copy = to(gath.at[part], gath.at[part], asend.at[i], arecv.at[i], wide=partner(b))
        copy.start()
        pending.append(copy)

    def ag_finish(h, s):
        st, b = state[h], orders[h][s]
        i = h * 2 * bits + bits + s
        there = st["off"] + (1 - 2 * bit_of(b)) * st["size"]
        part = pl.ds(mult8(there), st["size"])
        to(gath.at[part], gath.at[part], asend.at[i], arecv.at[i], wide=partner(b)).wait_recv()
        st.update(off=st["off"] - bit_of(b) * st["size"], size=st["size"] * 2)

    step = min(hrows, 256)
    for h in range(nh):
        for r in range(h * hrows, (h + 1) * hrows, step):
            fact[r : r + step, :] = jnp.dot(table[r : r + step, :], weighted, preferred_element_type=f32)
        rs_start(h, 0)

    def job_peer(s):
        def run():
            if s == 0:
                for i in range(N):
                    j = lax.rem(n + N - i, N)

                    @pl.when(has_next)
                    def _():
                        forward(i, j).wait_recv()

                @pl.when(jnp.logical_not(has_next))
                def _():
                    for i in range(N):
                        both[N + i] = jnp.zeros((B, C), f32)

            f_peer = both[list_ref[0, 1, 0, s] * N + list_ref[0, 2, 0, s]]
            for k in range(RBF):
                ypeer[k * B : (k + 1) * B, :] = (f_peer * wrbf_ref[k : k + 1, :]).astype(bf16)
            value = jnp.dot(gh[s], ypeer[...], preferred_element_type=f32)
            own_acc[...] = value if s == 0 else own_acc[...] + value

        return run

    def job_next():
        for copy in znext:
            copy.wait_recv()
        msum[...] = buf[N + n] + sb[1] + sb[2] + sb[3] if N == 4 else sum((sb[d] for d in range(1, N)), buf[N + n])

        @pl.when(has_next)
        def _():
            to(msum, msg, msend, mrecv, wide=nxt).start()

    jobs = [job_peer(s) for s in range(SLOTS)]
    for s in range(2 * bits):
        if jobs:
            jobs.pop(0)()
        for h in range(nh):
            if s < bits:
                rs_finish(h, s)
                if s < bits - 1:
                    rs_start(h, s + 1)
                else:
                    ag_start(h, bits - 1)
            else:
                a = 2 * bits - 1 - s
                ag_finish(h, a)
                if a > 0:
                    ag_start(h, a - 1)
    for job in jobs:
        job()
    job_next()

    atoms_all = B * N * W
    locals_[2].wait()
    for base in (0, qdev):
        filt[base : base + qdev, :] = (kf[...] * gath[base : base + qdev, :] / atoms_all).astype(bf16)

    last = []
    for d in (2, 1, 3) if N == 4 else range(1, N):
        j = lax.rem(n + d, N)
        fin[d] = buf[j] + jnp.dot(table_t[j], filt[...], preferred_element_type=f32)
        last.append(to(fin.at[d], fin.at[N + d], esend.at[d], erecv.at[d], narrow=j))
        last[-1].start()
    own = buf[n] + own_acc[...] + jnp.dot(table_t[n], filt[...], preferred_element_type=f32)

    @pl.when(has_prev)
    def _():
        to(msum, msg, msend, mrecv, wide=nxt).wait_recv()

    @pl.when(jnp.logical_not(has_prev))
    def _():
        msg[...] = jnp.zeros_like(msg)

    own = own + msg[...]
    locals_[3].wait()
    locals_[4].wait()
    for copy in last:
        copy.wait_recv()
    for d in range(1, N):
        own = own + fin[N + d]
    hidden = jnp.dot(own.astype(bf16), win[...], preferred_element_type=f32)
    hidden = (hidden / (1.0 + jnp.exp(-hidden))).astype(bf16)
    out_ref[...] = weight(n) * (both[n] + jnp.dot(hidden, wout[...], preferred_element_type=f32))

    for copy in pos_out + feat_out + znext + last + pending:
        copy.wait_send()

    @pl.when(has_prev)
    def _():
        pos_fwd.wait_send()
        for i in range(N):
            forward(i, lax.rem(n + N - i, N)).wait_send()

    @pl.when(has_next)
    def _():
        to(msum, msg, msend, mrecv, wide=nxt).wait_send()


def local(W, N, positions, features, block_counts, pair_list, pair_count, pair_mask, w_rbf, wavevectors, kfilter, w_in, w_out):
    B, C = features.shape
    RBF = w_rbf.shape[0]
    SLOTS = pair_list.shape[3]
    rows = 2 * wavevectors.shape[1]
    bits = W.bit_length() - 1
    vmem = pl.BlockSpec(memory_space=pltpu.VMEM)
    smem = pl.BlockSpec(memory_space=pltpu.SMEM)
    hbm = pl.BlockSpec(memory_space=pltpu.HBM)
    dma = pltpu.SemaphoreType.DMA
    V = pltpu.VMEM
    return pl.pallas_call(
        functools.partial(kernel, (W, N, B, C, RBF, SLOTS)),
        out_shape=jax.ShapeDtypeStruct((B, C), f32),
        in_specs=[smem] * 3 + [hbm] * 8,
        out_specs=vmem,
        scratch_shapes=[
            V(positions.shape, f32),
            V(w_rbf.shape, f32),
            V(wavevectors.shape, f32),
            V((2 * N, B, C), f32),
            V((2 * N, 3, B), f32),
            V((rows, N * B), bf16),
            V((N, B, rows), bf16),
            V((rows, C), f32),
            V((rows, C), f32),
            V((rows, C), f32),
            V((rows, C), bf16),
            V((SLOTS, B, RBF * B), bf16),
            V((SLOTS, B, RBF * B), bf16),
            V((RBF * B, C), bf16),
            V((RBF * B, C), bf16),
            V((SLOTS, B, C), f32),
            V((2 * N, B, C), f32),
            V((B, C), f32),
            V((3, B, B), f32),
            V((B, C), f32),
            V((B, C), f32),
            V((N, B, C), f32),
            V((2 * N, B, C), f32),
            V(pair_mask.shape[2:], jnp.int32),
            V(kfilter.shape, f32),
            V(w_in.shape, bf16),
            V(w_out.shape, bf16),
            dma((9,)),
            dma((N,)), dma((N,)),
            dma((N,)), dma((N,)),
            dma((N,)), dma((N,)),
            dma, dma,
            dma((2 * bits * CHAINS[0],)), dma((2 * bits * CHAINS[0],)),
            dma((N,)), dma((N,)),
            dma, dma,
            dma((N,)), dma((N,)),
        ],
        compiler_params=pltpu.CompilerParams(
            collective_id=0, has_side_effects=True, vmem_limit_bytes=67043328
        ),
    )(block_counts, jnp.transpose(pair_list, (0, 2, 1, 3)), pair_count, positions, w_rbf, wavevectors, features, pair_mask, kfilter, w_in, w_out)


def solution(mesh):
    placed = (
        P(None, ("wide", "narrow")),
        P(("wide", "narrow"), None),
        P("wide"),
        P("wide", "narrow", None, None),
        P("wide", "narrow"),
        P("wide", "narrow", None, None, None),
        P(),
        P(None, "narrow"),
        P("narrow", None),
        P(),
        P(),
    )
    body = functools.partial(local, mesh.shape["wide"], mesh.shape["narrow"])
    return jax.shard_map(
        body, mesh=mesh, in_specs=placed, out_specs=P(("wide", "narrow"), None), check_vma=False
    )
```

```python
import functools
import math

import jax
import jax.numpy as jnp
from jax import lax
from jax.experimental import pallas as pl
from jax.experimental.pallas import tpu as pltpu
from jax.sharding import PartitionSpec as P

cutoff = 2.0
sigma_width = 0.25
MESH = pl.DeviceIdType.MESH
CHAINS = (8, 4, 2, 1)
f32, bf16 = jnp.float32, jnp.bfloat16

COS = (1.0, -19.73920440673828, 64.93911743164062, -85.45014190673828,
       60.167633056640625, -25.967601776123047, 6.528658866882324)
SIN = (6.2831854820251465, -41.34170150756836, 81.60513305664062, -76.70301818847656,
       42.02592849731445, -14.899847984313965, 3.238137722015381)


def horner(coefs, u):
    acc = coefs[-1]
    for c in coefs[-2::-1]:
        acc = acc * u + c
    return acc


def column(row, size):
    return jnp.transpose(jnp.broadcast_to(row, (size, size)))


def kernel(
    cfg,
    cnt_ref, list_ref, pcount_ref,
    pos_hbm, wrbf_hbm, wv_hbm, feat_ref, mask_hbm, kf_hbm, win_hbm, wout_hbm,
    out_ref,
    pos_ref, wrbf_ref, wv_ref,
    both, bpos, table, table_t, fact, rbuf, gath, filt,
    gh, gt, yown, ypeer, tp, buf, own_acc, ncv, msg, msum, sb, fin,
    mask, kf, win, wout,
    lsem, psend, precv, fsend, frecv, nsend, nrecv, npsend, nprecv,
    asend, arecv, zsend, zrecv, msend, mrecv, esend, erecv,
):
    W, N, B, C, RBF, SLOTS = cfg
    w, n = lax.axis_index("wide"), lax.axis_index("narrow")
    bits = W.bit_length() - 1
    qdev = wv_ref.shape[1]
    rows = 2 * qdev

    locals_ = [
        pltpu.make_async_copy(feat_ref, both.at[n], lsem.at[0]),
        pltpu.make_async_copy(mask_hbm.at[0, 0], mask, lsem.at[1]),
        pltpu.make_async_copy(kf_hbm, kf, lsem.at[2]),
        pltpu.make_async_copy(win_hbm, win, lsem.at[3]),
        pltpu.make_async_copy(wout_hbm, wout, lsem.at[4]),
        pltpu.make_async_copy(pos_hbm, pos_ref, lsem.at[5]),
        pltpu.make_async_copy(wrbf_hbm, wrbf_ref, lsem.at[6]),
        pltpu.make_async_copy(wv_hbm, wv_ref, lsem.at[7]),
        pltpu.make_async_copy(pos_hbm, bpos.at[n], lsem.at[8]),
    ]
    for i in (5, 8, 7, 0, 6, 1, 2, 3, 4):
        locals_[i].start()

    barrier = pltpu.get_barrier_semaphore()
    partners = [dict(wide=w, narrow=lax.rem(n + d, N)) for d in range(1, N)]
    partners += [dict(wide=w + (1 - 2 * ((w // (1 << b)) % 2)) * (1 << b), narrow=n) for b in range(bits)]
    partners += [dict(wide=lax.rem(w + 1, W), narrow=n), dict(wide=lax.rem(w + W - 1, W), narrow=n)]
    for p in partners:
        pl.semaphore_signal(barrier, inc=1, device_id=p, device_id_type=MESH)
    pl.semaphore_wait(barrier, len(partners))

    def to(src, dst, ss, rs, **dev):
        ids = dict(wide=w, narrow=n)
        ids.update(dev)
        return pltpu.make_async_remote_copy(
            src_ref=src, dst_ref=dst, send_sem=ss, recv_sem=rs, device_id=ids, device_id_type=MESH
        )

    has_prev = w > 0
    has_next = w < W - 1
    prev = lax.rem(w + W - 1, W)
    nxt = lax.rem(w + 1, W)

    pos_out, feat_out = [], []
    for d in range(1, N):
        pos_out.append(to(pos_hbm, bpos.at[n], psend.at[d], precv.at[d], narrow=lax.rem(n + d, N)))
        pos_out[-1].start()
    for d in (2, 1, 3) if N == 4 else range(1, N):
        feat_out.append(to(feat_ref, both.at[n], fsend.at[d], frecv.at[d], narrow=lax.rem(n + d, N)))
        feat_out[-1].start()

    def forward(i, j):
        return to(both.at[j], both.at[N + j], nsend.at[i], nrecv.at[i], wide=prev)

    for i in (0, 5, 6, 7, 8):
        locals_[i].wait()

    @pl.when(has_prev)
    def _():
        forward(0, n).start()

    for d in range(1, N):
        src = lax.rem(n + N - d, N)
        to(pos_ref, bpos.at[src], psend.at[d], precv.at[d], narrow=src).wait_recv()
    pos_fwd = to(bpos.at[pl.ds(0, N)], bpos.at[pl.ds(N, N)], npsend, nprecv, wide=prev)

    @pl.when(has_prev)
    def _():
        pos_fwd.start()

    def wave_chunk(qc, _):
        q0 = pl.multiple_of(qc * B, B)
        wc = [column(wv_ref[i : i + 1, pl.ds(q0, B)] * (0.5 / math.pi), B) for i in range(3)]

        def atom_chunk(j, _):
            p = bpos[j]
            t = wc[0] * p[0:1] + wc[1] * p[1:2] + wc[2] * p[2:3]
            t = t - jnp.round(t)
            u = t * t
            for base, value in ((0, horner(COS, u)), (qdev, t * horner(SIN, u))):
                at = pl.multiple_of(base + q0, B)
                table[pl.ds(at, B), pl.ds(pl.multiple_of(j * B, B), B)] = value.astype(bf16)
                table_t[j, :, pl.ds(at, B)] = jnp.transpose(value).astype(bf16)
            return 0

        return lax.fori_loop(0, N, atom_chunk, 0)

    lax.fori_loop(0, qdev // B, wave_chunk, 0)

    f_own = both[n]
    for k in range(RBF):
        yown[k * B : (k + 1) * B, :] = (f_own * wrbf_ref[k : k + 1, :]).astype(bf16)

    @pl.when(has_next)
    def _():
        to(bpos.at[pl.ds(0, N)], bpos.at[pl.ds(N, N)], npsend, nprecv, wide=prev).wait_recv()

    @pl.when(jnp.logical_not(has_next))
    def _():
        bpos[pl.ds(N, N)] = jnp.zeros((N,) + bpos.shape[1:], f32)

    locals_[1].wait()
    alpha = math.sqrt(math.log2(math.e)) / sigma_width
    for i in range(3):
        ncv[i] = column(pos_ref[i : i + 1, :], B)

    def slot_filters(s, _):
        p = bpos[list_ref[0, 1, 0, s] * N + list_ref[0, 2, 0, s]]
        taken = jnp.where(s < pcount_ref[0, 0], 1.0, 0.0).astype(f32)
        dx, dy, dz = ncv[0] - p[0:1], ncv[1] - p[1:2], ncv[2] - p[2:3]
        squared = dx * dx + dy * dy + dz * dz
        dist = jnp.sqrt(squared + 0.01) * alpha
        env = 1.0 - jnp.minimum(squared * (1.0 / (cutoff * cutoff)), 1.0)
        em = env * env * (mask[s].astype(f32) * taken)
        dist_t, em_t = jnp.transpose(dist), jnp.transpose(em)
        for k in range(RBF):
            center = k * (cutoff / (RBF - 1)) * alpha
            a = dist - center
            b = dist_t - center
            gh[s, :, k * B : (k + 1) * B] = (jnp.exp2(-(a * a)) * em).astype(bf16)
            gt[s, :, k * B : (k + 1) * B] = (jnp.exp2(-(b * b)) * em_t).astype(bf16)
        return 0

    lax.fori_loop(0, SLOTS, slot_filters, 0)

    for s in range(SLOTS):
        tp[s] = jnp.dot(gt[s], yown[...], preferred_element_type=f32)

    def spread(j, _):
        acc = jnp.zeros((B, C), f32)
        for s in range(SLOTS):
            hit = (list_ref[0, 1, 0, s] * N + list_ref[0, 2, 0, s]) == j
            acc = acc + tp[s] * jnp.where(hit, 1.0, 0.0).astype(f32)
        buf[j] = acc
        return 0

    lax.fori_loop(0, 2 * N, spread, 0)

    znext = []
    for d in range(1, N):
        j = lax.rem(n + d, N)
        znext.append(to(buf.at[N + j], sb.at[d], zsend.at[d], zrecv.at[d], narrow=j))
        znext[-1].start()

    live = cnt_ref[0]

    def weight(j):
        return jnp.where(j < live, 1.0, 0.0).astype(f32)

    for i, d in enumerate((1, 2, 3) if N == 4 else range(1, N)):
        src = lax.rem(n + N - d, N)
        to(feat_ref, both.at[src], fsend.at[d], frecv.at[d], narrow=src).wait_recv()

        @pl.when(has_prev)
        def _():
            forward(d, src).start()

    weighted = jnp.concatenate([(both[j] * weight(j)).astype(bf16) for j in range(N)], axis=0)

    nh = next(c for c in CHAINS if rows % (c * 8 * W) == 0)
    hrows = rows // nh
    orders = [list(range(bits)) if h % 2 == 0 else [0] + list(range(bits - 1, 0, -1)) for h in range(nh)]

    def bit_of(b):
        return (w // (1 << b)) % 2

    def partner(b):
        return w + (1 - 2 * bit_of(b)) * (1 << b)

    state = [dict(off=h * hrows, size=hrows, at=h * hrows) for h in range(nh)]
    pending = []

    def mult8(x):
        return pl.multiple_of(x, 8)

    def rs_start(h, s):
        st, b = state[h], orders[h][s]
        half = st["size"] // 2
        mine = st["off"] + bit_of(b) * half
        other = st["off"] + (1 - bit_of(b)) * half
        i = h * 2 * bits + s
        copy = to(fact.at[pl.ds(mult8(other), half)], rbuf.at[pl.ds(st["at"], half)], asend.at[i], arecv.at[i], wide=partner(b))
        copy.start()
        pending.append(copy)
        st.update(copy=copy, off=mine, size=half)

    def rs_finish(h, s):
        st = state[h]
        st["copy"].wait_recv()
        part = pl.ds(mult8(st["off"]), st["size"])
        total = fact[part, :] + rbuf[pl.ds(st["at"], st["size"]), :]
        st["at"] += st["size"]
        if s == bits - 1:
            gath[part, :] = total
        else:
            fact[part, :] = total

    def ag_start(h, s):
        st, b = state[h], orders[h][s]
        part = pl.ds(mult8(st["off"]), st["size"])
        i = h * 2 * bits + bits + s
        copy = to(gath.at[part], gath.at[part], asend.at[i], arecv.at[i], wide=partner(b))
        copy.start()
        pending.append(copy)

    def ag_finish(h, s):
        st, b = state[h], orders[h][s]
        i = h * 2 * bits + bits + s
        there = st["off"] + (1 - 2 * bit_of(b)) * st["size"]
        part = pl.ds(mult8(there), st["size"])
        to(gath.at[part], gath.at[part], asend.at[i], arecv.at[i], wide=partner(b)).wait_recv()
        st.update(off=st["off"] - bit_of(b) * st["size"], size=st["size"] * 2)

    step = min(hrows, 256)
    for h in range(nh):
        for r in range(h * hrows, (h + 1) * hrows, step):
            fact[r : r + step, :] = jnp.dot(table[r : r + step, :], weighted, preferred_element_type=f32)
        rs_start(h, 0)

    def job_peer(s):
        def run():
            if s == 0:
                for i in range(N):
                    j = lax.rem(n + N - i, N)

                    @pl.when(has_next)
                    def _():
                        forward(i, j).wait_recv()

                @pl.when(jnp.logical_not(has_next))
                def _():
                    for i in range(N):
                        both[N + i] = jnp.zeros((B, C), f32)

            f_peer = both[list_ref[0, 1, 0, s] * N + list_ref[0, 2, 0, s]]
            for k in range(RBF):
                ypeer[k * B : (k + 1) * B, :] = (f_peer * wrbf_ref[k : k + 1, :]).astype(bf16)
            value = jnp.dot(gh[s], ypeer[...], preferred_element_type=f32)
            own_acc[...] = value if s == 0 else own_acc[...] + value

        return run

    def job_next():
        for copy in znext:
            copy.wait_recv()
        msum[...] = buf[N + n] + sb[1] + sb[2] + sb[3] if N == 4 else sum((sb[d] for d in range(1, N)), buf[N + n])

        @pl.when(has_next)
        def _():
            to(msum, msg, msend, mrecv, wide=nxt).start()

    jobs = [job_peer(s) for s in range(SLOTS)]
    for s in range(2 * bits):
        if jobs:
            jobs.pop(0)()
        for h in range(nh):
            if s < bits:
                rs_finish(h, s)
                if s < bits - 1:
                    rs_start(h, s + 1)
                else:
                    ag_start(h, bits - 1)
            else:
                a = 2 * bits - 1 - s
                ag_finish(h, a)
                if a > 0:
                    ag_start(h, a - 1)
    for job in jobs:
        job()
    job_next()

    atoms_all = B * N * W
    locals_[2].wait()
    for base in (0, qdev):
        filt[base : base + qdev, :] = (kf[...] * gath[base : base + qdev, :] * (1.0 / atoms_all)).astype(bf16)

    last = []
    for d in (2, 1, 3) if N == 4 else range(1, N):
        j = lax.rem(n + d, N)
        fin[d] = buf[j] + jnp.dot(table_t[j], filt[...], preferred_element_type=f32)
        last.append(to(fin.at[d], fin.at[N + d], esend.at[d], erecv.at[d], narrow=j))
        last[-1].start()
    own = buf[n] + own_acc[...] + jnp.dot(table_t[n], filt[...], preferred_element_type=f32)

    @pl.when(has_prev)
    def _():
        to(msum, msg, msend, mrecv, wide=nxt).wait_recv()

    @pl.when(jnp.logical_not(has_prev))
    def _():
        msg[...] = jnp.zeros_like(msg)

    own = own + msg[...]
    locals_[3].wait()
    locals_[4].wait()
    for copy in last:
        copy.wait_recv()
    for d in range(1, N):
        own = own + fin[N + d]
    hidden = jnp.dot(own.astype(bf16), win[...], preferred_element_type=f32)
    hidden = (hidden / (1.0 + jnp.exp(-hidden))).astype(bf16)
    out_ref[...] = weight(n) * (both[n] + jnp.dot(hidden, wout[...], preferred_element_type=f32))

    for copy in pos_out + feat_out + znext + last + pending:
        copy.wait_send()

    @pl.when(has_prev)
    def _():
        pos_fwd.wait_send()
        for i in range(N):
            forward(i, lax.rem(n + N - i, N)).wait_send()

    @pl.when(has_next)
    def _():
        to(msum, msg, msend, mrecv, wide=nxt).wait_send()


def local(W, N, positions, features, block_counts, pair_list, pair_count, pair_mask, w_rbf, wavevectors, kfilter, w_in, w_out):
    B, C = features.shape
    RBF = w_rbf.shape[0]
    SLOTS = pair_list.shape[3]
    rows = 2 * wavevectors.shape[1]
    bits = W.bit_length() - 1
    vmem = pl.BlockSpec(memory_space=pltpu.VMEM)
    smem = pl.BlockSpec(memory_space=pltpu.SMEM)
    hbm = pl.BlockSpec(memory_space=pltpu.HBM)
    dma = pltpu.SemaphoreType.DMA
    V = pltpu.VMEM
    return pl.pallas_call(
        functools.partial(kernel, (W, N, B, C, RBF, SLOTS)),
        out_shape=jax.ShapeDtypeStruct((B, C), f32),
        in_specs=[smem] * 3 + [hbm] * 8,
        out_specs=vmem,
        scratch_shapes=[
            V(positions.shape, f32),
            V(w_rbf.shape, f32),
            V(wavevectors.shape, f32),
            V((2 * N, B, C), f32),
            V((2 * N, 3, B), f32),
            V((rows, N * B), bf16),
            V((N, B, rows), bf16),
            V((rows, C), f32),
            V((rows, C), f32),
            V((rows, C), f32),
            V((rows, C), bf16),
            V((SLOTS, B, RBF * B), bf16),
            V((SLOTS, B, RBF * B), bf16),
            V((RBF * B, C), bf16),
            V((RBF * B, C), bf16),
            V((SLOTS, B, C), f32),
            V((2 * N, B, C), f32),
            V((B, C), f32),
            V((3, B, B), f32),
            V((B, C), f32),
            V((B, C), f32),
            V((N, B, C), f32),
            V((2 * N, B, C), f32),
            V(pair_mask.shape[2:], jnp.int32),
            V(kfilter.shape, f32),
            V(w_in.shape, bf16),
            V(w_out.shape, bf16),
            dma((9,)),
            dma((N,)), dma((N,)),
            dma((N,)), dma((N,)),
            dma((N,)), dma((N,)),
            dma, dma,
            dma((2 * bits * CHAINS[0],)), dma((2 * bits * CHAINS[0],)),
            dma((N,)), dma((N,)),
            dma, dma,
            dma((N,)), dma((N,)),
        ],
        compiler_params=pltpu.CompilerParams(
            collective_id=0, has_side_effects=True, vmem_limit_bytes=67043328
        ),
    )(block_counts, jnp.transpose(pair_list, (0, 2, 1, 3)), pair_count, positions, w_rbf, wavevectors, features, pair_mask, kfilter, w_in, w_out)


def solution(mesh):
    placed = (
        P(None, ("wide", "narrow")),
        P(("wide", "narrow"), None),
        P("wide"),
        P("wide", "narrow", None, None),
        P("wide", "narrow"),
        P("wide", "narrow", None, None, None),
        P(),
        P(None, "narrow"),
        P("narrow", None),
        P(),
        P(),
    )
    body = functools.partial(local, mesh.shape["wide"], mesh.shape["narrow"])
    return jax.shard_map(
        body, mesh=mesh, in_specs=placed, out_specs=P(("wide", "narrow"), None), check_vma=False
    )
```
